32 devices in a mesh: order: 2 (over core), tok: 16 (over z, y, x).
Axes of the slice: x: 2, y: 2, z: 4, core: 2. Of those that a mesh axis runs over, the one named last changes fastest.
Arguments:
- queries: bfloat16 [65536, 512], P(('order', 'tok')), may hold values from -6 to 6
- key_tokens: bfloat16 [65536, 512], P(('order', 'tok')), may hold values from -6 to 6
- value_tokens: bfloat16 [65536, 512], P(('order', 'tok')), may hold values from -6 to 6
- learn_rates: float32 [65536], P(('order', 'tok')), may hold values from 0.02 to 0.2
- fast_init: float32 [512, 1536], replicated, may hold values from -0.25 to 0.25
- out_gain: float32 [512], replicated, may hold values from 0.5 to 1.5
Outputs:
- output: bfloat16 [65536, 512], P(('order', 'tok'))
The draws below stay inside these ranges and needn't reach their ends.
All inputs are finite; a program needn't handle non-finite values.
Results may differ from the reference program's by a relative error of at most 0.015.
Values may be sent and summed in bfloat16 or wider, within the bound.
A program may use at most 128 MiB of HBM per device.

```python
import math
import jax
import jax.numpy as jnp
from jax import lax

D = 512
TOK_DEV = 2048
TOKENS = 65536
N_ORDER = 2
N_TOK = 16


def block_scale(stream_key, dims, split, smallest, largest):
    level = 1.0
    for position, shards_of in split:
        heights = jax.random.uniform(jax.random.fold_in(jax.random.fold_in(stream_key, 6), position), (shards_of,), jnp.float32, smallest / len(split), largest / len(split))
        level = level * jnp.repeat(jnp.exp(heights), dims[position] // shards_of).reshape((-1,) + (1,) * (len(dims) - 1 - position))
    return level


def normal_values(key, shape, scale, bound, split=(), kind=jnp.bfloat16):
    values = scale * jax.random.normal(key, shape, jnp.float32)
    if split:
        values = values * block_scale(key, shape, split, -0.22, 0.18)
    return jnp.clip(values, -bound, bound).astype(kind)


def setup_inputs(seed: int = 0) -> dict:
    streams_of = jax.random.split(jax.random.key(seed), 7)
    queries = normal_values(streams_of[0], (TOKENS, D), 1.0, 6.0, ((0, 32),))
    key_tokens = normal_values(streams_of[1], (TOKENS, D), 1.0, 6.0, ((0, 32),))
    value_tokens = normal_values(streams_of[2], (TOKENS, D), 1.0, 6.0, ((0, 32),))
    learn_rates = jnp.clip(jnp.exp(math.log(0.2) - 2.3025851 * jax.random.uniform(streams_of[3], (TOKENS,), jnp.float32) ** block_scale(streams_of[3], (TOKENS,), ((0, 32),), -0.2, 0.2)), 0.02, 0.2)
    fast_init = normal_values(streams_of[4], (D, 3 * D), D ** -0.5, 0.25, (), jnp.float32)
    out_gain = jnp.clip(1.0 + 0.1 * jax.random.normal(streams_of[5], (D,), jnp.float32), 0.5, 1.5)
    return {"queries": queries, "key_tokens": key_tokens, "value_tokens": value_tokens, "learn_rates": learn_rates, "fast_init": fast_init, "out_gain": out_gain}


def gate_up(rows_in, weights_bf):
    width = weights_bf.shape[0]
    both_parts = jnp.dot(rows_in, weights_bf[:, :2 * width], preferred_element_type=jnp.float32)
    return (both_parts[:, :width], both_parts[:, width:])

def gradient(key_rows, target, weights):
    width = weights.shape[0]
    weights_bf = weights.astype(jnp.bfloat16)
    gate_pre, up_pre = gate_up(key_rows, weights_bf)
    squash = jax.nn.sigmoid(gate_pre)
    activated = gate_pre * squash
    hidden = (activated * up_pre).astype(jnp.bfloat16)
    hidden_grad = lax.dot_general(target, weights_bf[:, 2 * width:], (((1,), (1,)), ((), ())), preferred_element_type=jnp.float32)
    gate_grad = (hidden_grad * up_pre * squash * (1.0 + gate_pre * (1.0 - squash))).astype(jnp.bfloat16)
    up_grad = (hidden_grad * activated).astype(jnp.bfloat16)
    inner_grads = jnp.concatenate([gate_grad, up_grad], axis=1)
    upper = lax.dot_general(key_rows, inner_grads, (((0,), (0,)), ((), ())), preferred_element_type=jnp.float32)
    lower = lax.dot_general(hidden, target, (((0,), (0,)), ((), ())), preferred_element_type=jnp.float32)
    return jnp.concatenate([upper, lower], axis=1)

def apply_weights(query_rows, closing, out_gain):
    width = closing.shape[0]
    weights_bf = closing.astype(jnp.bfloat16)
    gate_pre, up_pre = gate_up(query_rows, weights_bf)
    hidden = (jax.nn.silu(gate_pre) * up_pre).astype(jnp.bfloat16)
    result = jnp.dot(hidden, weights_bf[:, 2 * width:], preferred_element_type=jnp.float32)
    norm_inv = lax.rsqrt(lax.optimization_barrier(jnp.mean(result * result, axis=1, keepdims=True)) + 1e-06)
    return (result * norm_inv * out_gain[None, :]).astype(jnp.bfloat16)

def reference(queries, key_tokens, value_tokens, learn_rates, fast_init, out_gain):
    group_rows = TOK_DEV * N_TOK
    factor = group_rows ** (-0.5)
    changes = []
    for group_index in range(N_ORDER):
        low = group_index * group_rows
        key_rows = key_tokens[low:low + group_rows]
        target = (-(learn_rates[low:low + group_rows, None] * factor) * value_tokens[low:low + group_rows].astype(jnp.float32)).astype(jnp.bfloat16)
        first_step = fast_init - gradient(key_rows, target, fast_init)
        second_step = first_step - gradient(key_rows, target, first_step)
        changes.append(second_step - fast_init)
    outputs = []
    earlier = jnp.zeros_like(fast_init)
    for group_index in range(N_ORDER):
        low = group_index * group_rows
        closing = fast_init + earlier + changes[group_index]
        outputs.append(apply_weights(queries[low:low + group_rows], closing, out_gain))
        earlier = earlier + changes[group_index]
    return jnp.concatenate(outputs, axis=0)
```

```python
import functools

import jax
import jax.numpy as jnp
from jax import lax
from jax.experimental import pallas as pl
from jax.experimental.pallas import tpu as pltpu
from jax.sharding import PartitionSpec as P

CHUNKS = 2
PARTS = 4
MESH = pl.DeviceIdType.MESH


def prefix(x, axis, join, neutral):
    place = lax.axis_index(axis)
    gathered = lax.all_gather(x.astype(jnp.bfloat16), axis)
    state = jnp.zeros_like(x) + jnp.asarray(neutral, x.dtype)

    def one(lap, state):
        return join(state, lax.dynamic_index_in_dim(gathered, lap, 0, False).astype(x.dtype))

    return lax.fori_loop(0, place, one, state)


def gate_up(rows_in, weights_bf):
    width = weights_bf.shape[0]
    both_parts = jnp.dot(rows_in, weights_bf[:, : 2 * width], preferred_element_type=jnp.float32)
    return (both_parts[:, :width], both_parts[:, width:])


def backward_terms(key_rows, target, weights_bf):
    width = weights_bf.shape[0]
    gate_pre, up_pre = gate_up(key_rows, weights_bf)
    squash = jax.nn.sigmoid(gate_pre)
    activated = gate_pre * squash
    hidden = (activated * up_pre).astype(jnp.bfloat16)
    hidden_grad = lax.dot_general(
        target,
        weights_bf[:, 2 * width :],
        (((1,), (1,)), ((), ())),
        preferred_element_type=jnp.float32,
    )
    gate_grad = (hidden_grad * up_pre * squash * (1.0 + gate_pre * (1.0 - squash))).astype(
        jnp.bfloat16
    )
    up_grad = (hidden_grad * activated).astype(jnp.bfloat16)
    return (hidden, jnp.concatenate([gate_grad, up_grad], axis=1))


def local_term(key_rows, hidden, inner_grads, target):
    upper = lax.dot_general(
        key_rows, inner_grads, (((0,), (0,)), ((), ())), preferred_element_type=jnp.float32
    )
    lower = lax.dot_general(
        hidden, target, (((0,), (0,)), ((), ())), preferred_element_type=jnp.float32
    )
    return jnp.concatenate([upper, lower], axis=1)


def summed_whole(key_rows, target, weights_bf):
    hidden, inner_grads = backward_terms(key_rows, target, weights_bf)
    return lax.psum(local_term(key_rows, hidden, inner_grads, target), "tok")


def accumulate(earlier, later):
    return earlier + later


def apply_weights(query_rows, weights_bf, out_gain):
    width = weights_bf.shape[0]
    gate_pre, up_pre = gate_up(query_rows, weights_bf)
    hidden = (jax.nn.silu(gate_pre) * up_pre).astype(jnp.bfloat16)
    result = jnp.dot(hidden, weights_bf[:, 2 * width :], preferred_element_type=jnp.float32)
    norm_inv = lax.rsqrt(jnp.mean(result * result, axis=1, keepdims=True) + 1e-06)
    return (result * norm_inv * out_gain[None, :]).astype(jnp.bfloat16)


def shards(queries, key_tokens, value_tokens, learn_rates, fast_init, out_gain):
    group_rows = key_tokens.shape[0] * lax.axis_size("tok")
    factor = group_rows ** (-0.5)
    target = (-(learn_rates[:, None] * factor) * value_tokens.astype(jnp.float32)).astype(
        jnp.bfloat16
    )
    first_step = fast_init - summed_whole(key_tokens, target, fast_init.astype(jnp.bfloat16))
    second_step = first_step - summed_whole(key_tokens, target, first_step.astype(jnp.bfloat16))
    change = second_step - fast_init
    earlier = prefix(change, "order", accumulate, jnp.zeros_like(change))
    closing_bf = (fast_init + earlier + change).astype(jnp.bfloat16)
    return apply_weights(queries, closing_bf, out_gain)


def tiles(mesh):
    return mesh.shape["order"] == 2 and mesh.shape["tok"] == 16


def plan():
    compute = {"T": 1.0, "E": 0.9, "G": 0.8, "Q": 0.9}
    wire = {"x": 0.0, "y": 0.0, "z": 0.0}
    order, now = [], 0.0
    ready, done = {}, set()
    todo = []
    for step in range(2):
        for c in range(CHUNKS):
            for part in range(PARTS):
                todo.append(("E", step, c, part))
            for m in (2, 0, 1):
                todo.append(("G", step, c, m))
    for c in range(CHUNKS):
        for part in range(PARTS):
            todo.append(("Q", 2, c, part))

    def sent(links, us, latency):
        arrive = 0.0
        for link in links:
            wire[link] = max(wire[link], now) + us
            arrive = max(arrive, wire[link])
        return arrive + latency

    def blocked(op):
        if op[0] == "G" or op[1] == 0:
            return False
        return not all((op[1] - 1, op[2], m) in done for m in range(3))

    last = {0: 6, 1: 7}
    while todo or ready:
        due = sorted((when, key) for key, when in ready.items() if when <= now + 0.05)
        if due:
            key = due[0][1]
            piece, stage = key[:3], key[3]
            order.append(("S",) + key)
            del ready[key]
            now += 0.15
            name = STAGES[piece[0]][stage]
            if stage + 1 == len(STAGES[piece[0]]):
                done.add(piece)
                continue
            us, lat, links = COST[name]
            ready[piece + (stage + 1,)] = sent(links, us, lat)
            continue
        if todo and not blocked(todo[0]):
            op = todo.pop(0)
            order.append(op)
            now += compute[op[0]]
            if op[0] == "G":
                us, lat, links = COST["send1"]
                ready[(op[1], op[2], op[3], 0)] = sent(links, us, lat)
            continue
        now = max(now, min(ready.values()))
    return order


STAGES = (
    ("send2", "send3", "gather3", "gather2", "gather1", "end"),
    ("send2", "send3", "change", "gather3", "gather2", "gather1", "end"),
)
COST = {
    "send1": (1.4, 1.8, "xy"),
    "send2": (0.7, 1.8, "xy"),
    "send3": (1.4, 3.2, "z"),
    "change": (0.0, 1.2, ""),
    "gather3": (1.4, 3.2, "z"),
    "gather2": (0.7, 1.8, "xy"),
    "gather1": (1.4, 1.8, "xy"),
}


def fused_kernel(
    factor, key_ref, value_ref, rate_ref, init_ref, gain_ref, query_hbm, out_ref,
    key_t, target, target_t, terms, weights, shard, init_down, grad, grad_bf,
    part2, part2_bf, part3_bf, got1, got2, got3, change_mine, change_got,
    query, y_part, query_sem, send_sem, recv_sem,
):
    me, place = lax.axis_index("tok"), lax.axis_index("order")
    x, y, z = me % 2, (me // 2) % 2, me // 4
    n_z = got3.shape[3] + 1
    by_x = me + 1 - 2 * x
    by_y = me + 2 - 4 * y
    far = [((z + d) % n_z) for d in range(1, n_z)]
    by_z = [zz * 4 + me % 4 for zz in far]
    barrier = pltpu.get_barrier_semaphore()
    for peer in [by_x, by_y] + by_z:
        pl.semaphore_signal(barrier, inc=1, device_id={"tok": peer}, device_id_type=MESH)
    pl.semaphore_signal(barrier, inc=1, device_id={"order": 1 - place}, device_id_type=MESH)

    width = key_ref.shape[1]
    cols = width // CHUNKS
    rows = key_ref.shape[0] // PARTS
    half = width // 2
    fetch = pltpu.make_async_copy(query_hbm, query, query_sem)
    fetch.start()

    first, second = (x, y), (y, x)
    peer1, peer2 = (by_x, by_y), (by_y, by_x)
    r128 = half // 2
    r64 = half // 4
    r16 = r64 // n_z
    own1 = [h * half + first[h] * r128 for h in range(2)]
    off1 = [h * half + (1 - first[h]) * r128 for h in range(2)]
    own2 = [own1[h] + second[h] * r64 for h in range(2)]
    own3 = [own2[h] + z * r16 for h in range(2)]

    def at(start, size):
        return pl.ds(pl.multiple_of(start, size), size)

    for c in range(CHUNKS):
        here = slice(c * cols, (c + 1) * cols)
        for m in range(2):
            there = slice(m * width + c * cols, m * width + (c + 1) * cols)
            weights[0, c, m] = init_ref[:, there].astype(jnp.bfloat16)
        down_t = init_ref[here, 2 * width :].T
        init_down[c] = down_t
        weights[0, c, 2] = down_t.astype(jnp.bfloat16)

    def initial(c, m, h):
        if m == 2:
            return init_down[c, at(own3[h], r16), :]
        return init_ref[at(own3[h], r16), m * width + c * cols : m * width + (c + 1) * cols]

    def prepare(part):
        lines = slice(part * rows, (part + 1) * rows)
        key_t[:, lines] = key_ref[lines, :].T
        for b in range(part * rows // 128, (part + 1) * rows // 128):
            here = slice(b * 128, (b + 1) * 128)
            scale = -(jnp.broadcast_to(rate_ref[b : b + 1, :], (128, 128)).T * factor)
            for lane in range(0, width, 128):
                block = value_ref[here, lane : lane + 128].astype(jnp.float32)
                target[here, lane : lane + 128] = (scale * block).astype(jnp.bfloat16)
        target_t[:, lines] = target[lines, :].T

    def elementwise(step, c, part):
        if step == 0 and c == 0:
            prepare(part)
        lines = slice(part * rows, (part + 1) * rows)
        key_rows = key_ref[lines, :]
        gate = jnp.dot(key_rows, weights[step, c, 0], preferred_element_type=jnp.float32)
        up = jnp.dot(key_rows, weights[step, c, 1], preferred_element_type=jnp.float32)
        back = jnp.dot(target[lines, :], weights[step, c, 2], preferred_element_type=jnp.float32)
        sig = jax.nn.sigmoid(gate)
        act = gate * sig
        terms[2, lines, :] = (act * up).astype(jnp.bfloat16)
        terms[0, lines, :] = (back * up * sig * (1.0 + gate * (1.0 - sig))).astype(jnp.bfloat16)
        terms[1, lines, :] = (back * act).astype(jnp.bfloat16)

    def remote(src, dst, slot, device):
        copy = pltpu.make_async_remote_copy(
            src_ref=src, dst_ref=dst, send_sem=send_sem.at[slot], recv_sem=recv_sem.at[slot],
            device_id=device, device_id_type=MESH,
        )
        copy.start()
        return copy

    flying = {}
    greeted = []

    def slot_of(c, m, k):
        return (c * 3 + m) * (8 + 4 * n_z) + k

    def gradient(step, c, m):
        left = target_t if m == 2 else key_t
        total = jnp.dot(left[...], terms[m], preferred_element_type=jnp.float32)
        p = c * 3 + m
        grad[p] = total
        grad_bf[p] = total.astype(jnp.bfloat16)
        if not greeted:
            pl.semaphore_wait(barrier, 3 + len(far))
            greeted.append(True)
        flying[c, m] = [
            remote(grad_bf.at[p, at(off1[h], r128), :], got1.at[step, p, h],
                   slot_of(c, m, h), {"tok": peer1[h]})
            for h in range(2)
        ]

    def spread3(c, m, base, source, goal):
        return [
            remote(source(h, d), goal(h, d), slot_of(c, m, base + h * (n_z - 1) + d), {"tok": by_z[d]})
            for h in range(2)
            for d in range(n_z - 1)
        ]

    def advance(step, c, m, stage):
        p = c * 3 + m
        name = STAGES[step][stage]
        for copy in flying.pop((c, m)):
            copy.wait()
        held = weights.at[step + 1, c, m]
        if name == "send2":
            for h in range(2):
                mine, other = second[h] * r64, (1 - second[h]) * r64
                part2_bf[p, h] = (
                    grad[p, at(own1[h] + other, r64), :] + got1[step, p, h, at(other, r64), :].astype(jnp.float32)
                ).astype(jnp.bfloat16)
                part2[p, h] = grad[p, at(own2[h], r64), :] + got1[step, p, h, at(mine, r64), :].astype(jnp.float32)
            flying[c, m] = [
                remote(part2_bf.at[p, h], got2.at[step, p, h], slot_of(c, m, 2 + h), {"tok": peer2[h]})
                for h in range(2)
            ]
        elif name == "send3":
            for h in range(2):
                total = part2[p, h] + got2[step, p, h].astype(jnp.float32)
                part2[p, h] = total
                part3_bf[p, h] = total.astype(jnp.bfloat16)
            flying[c, m] = spread3(
                c, m, 4,
                lambda h, d: part3_bf.at[p, h, at(far[d] * r16, r16), :],
                lambda h, d: got3.at[step, p, h, d],
            )
        elif name == "change" or (name == "gather3" and step == 0):
            for h in range(2):
                total = part2[p, h, at(z * r16, r16), :]
                for d in range(n_z - 1):
                    total = total + got3[step, p, h, d].astype(jnp.float32)
                if step == 0:
                    fresh = initial(c, m, h) - total
                    shard[p, h] = fresh
                    weights[1, c, m, at(own3[h], r16), :] = fresh.astype(jnp.bfloat16)
                else:
                    change_mine[p, h] = (shard[p, h] - total) - initial(c, m, h)
            if step == 1:
                flying[c, m] = [
                    remote(change_mine.at[p], change_got.at[p], slot_of(c, m, 4 + 4 * n_z), {"order": 1 - place})
                ]
        if name == "gather3":
            if step == 1:
                for h in range(2):
                    earlier = jnp.where(place > 0, change_got[p, h], 0.0)
                    closing = initial(c, m, h) + earlier + change_mine[p, h]
                    weights[2, c, m, at(own3[h], r16), :] = closing.astype(jnp.bfloat16)
            flying[c, m] = spread3(
                c, m, 4 + 2 * (n_z - 1),
                lambda h, d: held.at[at(own3[h], r16), :],
                lambda h, d: held.at[at(own3[h], r16), :],
            )
        elif name in ("gather2", "gather1"):
            wide = name == "gather1"
            start, size = (own1, r128) if wide else (own2, r64)
            peer = peer1 if wide else peer2
            base = 4 + 4 * (n_z - 1) + (2 if wide else 0)
            flying[c, m] = [
                remote(held.at[at(start[h], size), :], held.at[at(start[h], size), :],
                       slot_of(c, m, base + h), {"tok": peer[h]})
                for h in range(2)
            ]

    def apply(step, c, part):
        if c == 0 and part == 0:
            fetch.wait()
        lines = slice(part * rows, (part + 1) * rows)
        rows_in = query[lines, :]
        gate = jnp.dot(rows_in, weights[step, c, 0], preferred_element_type=jnp.float32)
        up = jnp.dot(rows_in, weights[step, c, 1], preferred_element_type=jnp.float32)
        hidden = (jax.nn.silu(gate) * up).astype(jnp.bfloat16)
        result = lax.dot_general(
            hidden, weights[step, c, 2], (((1,), (1,)), ((), ())), preferred_element_type=jnp.float32
        )
        if c > 0:
            result = y_part[lines, :] + result
        if c < CHUNKS - 1:
            y_part[lines, :] = result
            return
        norm_inv = lax.rsqrt(jnp.mean(result * result, axis=1, keepdims=True) + 1e-06)
        out_ref[lines, :] = (result * norm_inv * gain_ref[...]).astype(jnp.bfloat16)

    for op in plan():
        {"E": elementwise, "G": gradient, "S": advance, "Q": apply}[op[0]](*op[1:])


def fused(queries, key_tokens, value_tokens, learn_rates, fast_init, out_gain):
    tokens, width = key_tokens.shape
    n_tok = lax.axis_size("tok")
    n_z = n_tok // 4
    cols = width // CHUNKS
    pieces = 3 * CHUNKS
    q = width // 8
    bf, f32 = jnp.bfloat16, jnp.float32
    factor = (tokens * n_tok) ** (-0.5)
    sems = pieces * (8 + 4 * n_z)
    vmem = pl.BlockSpec(memory_space=pltpu.VMEM)
    return pl.pallas_call(
        functools.partial(fused_kernel, factor),
        out_shape=jax.ShapeDtypeStruct((tokens, width), bf),
        in_specs=[vmem] * 5 + [pl.BlockSpec(memory_space=pl.ANY)],
        out_specs=vmem,
        scratch_shapes=[
            pltpu.VMEM((width, tokens), bf),
            pltpu.VMEM((tokens, width), bf),
            pltpu.VMEM((width, tokens), bf),
            pltpu.VMEM((3, tokens, cols), bf),
            pltpu.VMEM((3, CHUNKS, 3, width, cols), bf),
            pltpu.VMEM((pieces, 2, q // n_z, cols), f32),
            pltpu.VMEM((CHUNKS, width, cols), f32),
            pltpu.VMEM((pieces, width, cols), f32),
            pltpu.VMEM((pieces, width, cols), bf),
            pltpu.VMEM((pieces, 2, q, cols), f32),
            pltpu.VMEM((pieces, 2, q, cols), bf),
            pltpu.VMEM((pieces, 2, q, cols), bf),
            pltpu.VMEM((2, pieces, 2, 2 * q, cols), bf),
            pltpu.VMEM((2, pieces, 2, q, cols), bf),
            pltpu.VMEM((2, pieces, 2, n_z - 1, q // n_z, cols), bf),
            pltpu.VMEM((pieces, 2, q // n_z, cols), f32),
            pltpu.VMEM((pieces, 2, q // n_z, cols), f32),
            pltpu.VMEM((tokens, width), bf),
            pltpu.VMEM((tokens, width), f32),
            pltpu.SemaphoreType.DMA,
            pltpu.SemaphoreType.DMA((sems,)),
            pltpu.SemaphoreType.DMA((sems,)),
        ],
        compiler_params=pltpu.CompilerParams(
            collective_id=0, has_side_effects=True, vmem_limit_bytes=67043328
        ),
    )(
        key_tokens, value_tokens, learn_rates.reshape(-1, 128), fast_init,
        out_gain.reshape(1, -1), queries,
    )


def solution(mesh):
    return jax.shard_map(
        fused if tiles(mesh) else shards,
        mesh=mesh,
        in_specs=(
            P(("order", "tok"), None),
            P(("order", "tok"), None),
            P(("order", "tok"), None),
            P(("order", "tok")),
            P(),
            P(),
        ),
        out_specs=P(("order", "tok"), None),
        check_vma=False,
    )
```

```python
import functools

import jax
import jax.numpy as jnp
from jax import lax
from jax.experimental import pallas as pl
from jax.experimental.pallas import tpu as pltpu
from jax.sharding import PartitionSpec as P

CHUNKS = 4
PARTS = 4
MESH = pl.DeviceIdType.MESH


def prefix(x, axis, join, neutral):
    place = lax.axis_index(axis)
    gathered = lax.all_gather(x.astype(jnp.bfloat16), axis)
    state = jnp.zeros_like(x) + jnp.asarray(neutral, x.dtype)

    def one(lap, state):
        return join(state, lax.dynamic_index_in_dim(gathered, lap, 0, False).astype(x.dtype))

    return lax.fori_loop(0, place, one, state)


def gate_up(rows_in, weights_bf):
    width = weights_bf.shape[0]
    both_parts = jnp.dot(rows_in, weights_bf[:, : 2 * width], preferred_element_type=jnp.float32)
    return (both_parts[:, :width], both_parts[:, width:])


def backward_terms(key_rows, target, weights_bf):
    width = weights_bf.shape[0]
    gate_pre, up_pre = gate_up(key_rows, weights_bf)
    squash = jax.nn.sigmoid(gate_pre)
    activated = gate_pre * squash
    hidden = (activated * up_pre).astype(jnp.bfloat16)
    hidden_grad = lax.dot_general(
        target,
        weights_bf[:, 2 * width :],
        (((1,), (1,)), ((), ())),
        preferred_element_type=jnp.float32,
    )
    gate_grad = (hidden_grad * up_pre * squash * (1.0 + gate_pre * (1.0 - squash))).astype(
        jnp.bfloat16
    )
    up_grad = (hidden_grad * activated).astype(jnp.bfloat16)
    return (hidden, jnp.concatenate([gate_grad, up_grad], axis=1))


def local_term(key_rows, hidden, inner_grads, target):
    upper = lax.dot_general(
        key_rows, inner_grads, (((0,), (0,)), ((), ())), preferred_element_type=jnp.float32
    )
    lower = lax.dot_general(
        hidden, target, (((0,), (0,)), ((), ())), preferred_element_type=jnp.float32
    )
    return jnp.concatenate([upper, lower], axis=1)


def summed_whole(key_rows, target, weights_bf):
    hidden, inner_grads = backward_terms(key_rows, target, weights_bf)
    return lax.psum(local_term(key_rows, hidden, inner_grads, target), "tok")


def accumulate(earlier, later):
    return earlier + later


def apply_weights(query_rows, weights_bf, out_gain):
    width = weights_bf.shape[0]
    gate_pre, up_pre = gate_up(query_rows, weights_bf)
    hidden = (jax.nn.silu(gate_pre) * up_pre).astype(jnp.bfloat16)
    result = jnp.dot(hidden, weights_bf[:, 2 * width :], preferred_element_type=jnp.float32)
    norm_inv = lax.rsqrt(jnp.mean(result * result, axis=1, keepdims=True) + 1e-06)
    return (result * norm_inv * out_gain[None, :]).astype(jnp.bfloat16)


def shards(queries, key_tokens, value_tokens, learn_rates, fast_init, out_gain):
    group_rows = key_tokens.shape[0] * lax.axis_size("tok")
    factor = group_rows ** (-0.5)
    target = (-(learn_rates[:, None] * factor) * value_tokens.astype(jnp.float32)).astype(
        jnp.bfloat16
    )
    first_step = fast_init - summed_whole(key_tokens, target, fast_init.astype(jnp.bfloat16))
    second_step = first_step - summed_whole(key_tokens, target, first_step.astype(jnp.bfloat16))
    change = second_step - fast_init
    earlier = prefix(change, "order", accumulate, jnp.zeros_like(change))
    closing_bf = (fast_init + earlier + change).astype(jnp.bfloat16)
    return apply_weights(queries, closing_bf, out_gain)


def tiles(mesh):
    return mesh.shape["order"] == 2 and mesh.shape["tok"] == 16


def plan():
    compute = {"E": 0.6, "G": 1.0, "Q": 0.6}
    wire = {"x": 0.0, "y": 0.0, "z": 0.0}
    order, now = [], 0.0
    ready, done = {}, set()
    todo = []
    for step in range(2):
        for c in range(CHUNKS):
            for part in range(PARTS):
                todo.append(("E", step, c, part))
            todo.append(("G", step, c))
    for c in range(CHUNKS):
        for part in range(PARTS):
            todo.append(("Q", 2, c, part))

    def sent(links, us, latency):
        arrive = 0.0
        for link in links:
            wire[link] = max(wire[link], now) + us
            arrive = max(arrive, wire[link])
        return arrive + latency

    def blocked(op):
        if op[0] == "G" or op[1] == 0:
            return False
        return (op[1] - 1, op[2]) not in done

    while todo or ready:
        due = sorted((when, key) for key, when in ready.items() if when <= now + 0.05)
        if due:
            key = due[0][1]
            piece, stage = key[:2], key[2]
            order.append(("S",) + key)
            del ready[key]
            now += 0.15
            name = STAGES[piece[0]][stage]
            if stage + 1 == len(STAGES[piece[0]]):
                done.add(piece)
                continue
            us, lat, links = COST[name]
            ready[piece + (stage + 1,)] = sent(links, us, lat)
            continue
        if todo and not blocked(todo[0]):
            op = todo.pop(0)
            order.append(op)
            now += compute[op[0]]
            if op[0] == "G":
                us, lat, links = COST["send1"]
                ready[(op[1], op[2], 0)] = sent(links, us, lat)
            continue
        now = max(now, min(ready.values()))
    return order


STAGES = (
    ("send2", "send3", "gather3", "gather2", "gather1", "end"),
    ("send2", "send3", "change", "gather3", "gather2", "gather1", "end"),
)
COST = {
    "send1": (2.1, 2.2, "xy"),
    "send2": (1.0, 2.2, "xy"),
    "send3": (2.1, 3.6, "z"),
    "change": (0.0, 1.4, ""),
    "gather3": (2.1, 3.6, "z"),
    "gather2": (1.0, 2.2, "xy"),
    "gather1": (2.1, 2.2, "xy"),
}


def fused_kernel(
    factor, key_hbm, value_hbm, rate_ref, init_hbm, gain_ref, query_hbm, out_ref,
    key_t, target, target_t, terms, weights, shard, init_down, grad, grad_bf,
    part2, part2_bf, part3_bf, got1, got2, got3, change_mine, change_got,
    key_ref, value_ref, init_ref, query, y_part, load_sem, send_sem, recv_sem,
):
    me, place = lax.axis_index("tok"), lax.axis_index("order")
    x, y, z = me % 2, (me // 2) % 2, me // 4
    n_z = got3.shape[3] + 1
    by_x = me + 1 - 2 * x
    by_y = me + 2 - 4 * y
    far = [((z + d) % n_z) for d in range(1, n_z)]
    by_z = [zz * 4 + me % 4 for zz in far]
    barrier = pltpu.get_barrier_semaphore()
    for peer in [by_x, by_y] + by_z:
        pl.semaphore_signal(barrier, inc=1, device_id={"tok": peer}, device_id_type=MESH)
    pl.semaphore_signal(barrier, inc=1, device_id={"order": 1 - place}, device_id_type=MESH)

    width = key_ref.shape[1]
    cols = width // CHUNKS
    rows = key_ref.shape[0] // PARTS
    half = width // 2
    loads = []

    def load(src, dst):
        loads.append(pltpu.make_async_copy(src, dst, load_sem.at[len(loads)]))
        loads[-1].start()

    load(init_hbm, init_ref)
    for part in range(PARTS):
        lines = slice(part * rows, (part + 1) * rows)
        load(key_hbm.at[lines], key_ref.at[lines])
        load(value_hbm.at[lines], value_ref.at[lines])
    loads[0].wait()

    first, second = (x, y), (y, x)
    peer1, peer2 = (by_x, by_y), (by_y, by_x)
    r128 = half // 2
    r64 = half // 4
    r16 = r64 // n_z
    own1 = [h * half + first[h] * r128 for h in range(2)]
    off1 = [h * half + (1 - first[h]) * r128 for h in range(2)]
    own2 = [own1[h] + second[h] * r64 for h in range(2)]
    own3 = [own2[h] + z * r16 for h in range(2)]

    def at(start, size):
        return pl.ds(pl.multiple_of(start, size), size)

    def cast(c):
        here = slice(c * cols, (c + 1) * cols)
        for m in range(2):
            there = slice(m * width + c * cols, m * width + (c + 1) * cols)
            weights[0, c, :, m * cols : (m + 1) * cols] = init_ref[:, there].astype(jnp.bfloat16)
        down_t = init_ref[here, 2 * width :].T
        init_down[c] = down_t
        weights[0, c, :, 2 * cols :] = down_t.astype(jnp.bfloat16)

    def initial(c, h):
        mine = at(own3[h], r16)
        return jnp.concatenate(
            [
                init_ref[mine, c * cols : (c + 1) * cols],
                init_ref[mine, width + c * cols : width + (c + 1) * cols],
                init_down[c, mine, :],
            ],
            axis=1,
        )

    def prepare(part):
        lines = slice(part * rows, (part + 1) * rows)
        key_t[:, lines] = key_ref[lines, :].T
        for b in range(part * rows // 128, (part + 1) * rows // 128):
            here = slice(b * 128, (b + 1) * 128)
            scale = -(jnp.broadcast_to(rate_ref[b : b + 1, :], (128, 128)).T * factor)
            for lane in range(0, width, 128):
                block = value_ref[here, lane : lane + 128].astype(jnp.float32)
                target[here, lane : lane + 128] = (scale * block).astype(jnp.bfloat16)
        target_t[:, lines] = target[lines, :].T

    def elementwise(step, c, part):
        if step == 0 and part == 0:
            cast(c)
        if step == 0 and c == 0:
            loads[1 + 2 * part].wait()
            loads[2 + 2 * part].wait()
            prepare(part)
            if part == PARTS - 1:
                load(query_hbm, query)
        lines = slice(part * rows, (part + 1) * rows)
        key_rows = key_ref[lines, :]
        both = jnp.dot(key_rows, weights[step, c, :, : 2 * cols], preferred_element_type=jnp.float32)
        gate, up = both[:, :cols], both[:, cols:]
        back = jnp.dot(
            target[lines, :], weights[step, c, :, 2 * cols :], preferred_element_type=jnp.float32
        )
        sig = jax.nn.sigmoid(gate)
        act = gate * sig
        slope = back * up * sig * (1.0 + gate * (1.0 - sig))
        terms[lines, :cols] = slope.astype(jnp.bfloat16)
        terms[lines, cols : 2 * cols] = (back * act).astype(jnp.bfloat16)
        terms[lines, 2 * cols :] = (act * up).astype(jnp.bfloat16)

    def remote(src, dst, slot, device):
        copy = pltpu.make_async_remote_copy(
            src_ref=src, dst_ref=dst, send_sem=send_sem.at[slot], recv_sem=recv_sem.at[slot],
            device_id=device, device_id_type=MESH,
        )
        copy.start()
        return copy

    flying = {}
    greeted = []

    def slot_of(c, k):
        return c * (8 + 4 * n_z) + k

    def gradient(step, c):
        upper = jnp.dot(key_t[...], terms[:, : 2 * cols], preferred_element_type=jnp.float32)
        lower = jnp.dot(target_t[...], terms[:, 2 * cols :], preferred_element_type=jnp.float32)
        p = c
        grad[p, :, : 2 * cols] = upper
        grad[p, :, 2 * cols :] = lower
        grad_bf[p, :, : 2 * cols] = upper.astype(jnp.bfloat16)
        grad_bf[p, :, 2 * cols :] = lower.astype(jnp.bfloat16)
        if not greeted:
            pl.semaphore_wait(barrier, 3 + len(far))
            greeted.append(True)
        flying[c] = [
            remote(grad_bf.at[p, at(off1[h], r128), :], got1.at[step, p, h],
                   slot_of(c, h), {"tok": peer1[h]})
            for h in range(2)
        ]

    def spread3(c, base, source, goal):
        return [
            remote(source(h, d), goal(h, d), slot_of(c, base + h * (n_z - 1) + d), {"tok": by_z[d]})
            for h in range(2)
            for d in range(n_z - 1)
        ]

    def advance(step, c, stage):
        p = c
        name = STAGES[step][stage]
        for copy in flying.pop(c):
            copy.wait()
        held = weights.at[step + 1, c]
        if name == "send2":
            for h in range(2):
                mine, other = second[h] * r64, (1 - second[h]) * r64
                part2_bf[p, h] = (
                    grad[p, at(own1[h] + other, r64), :] + got1[step, p, h, at(other, r64), :].astype(jnp.float32)
                ).astype(jnp.bfloat16)
                part2[p, h] = grad[p, at(own2[h], r64), :] + got1[step, p, h, at(mine, r64), :].astype(jnp.float32)
            flying[c] = [
                remote(part2_bf.at[p, h], got2.at[step, p, h], slot_of(c, 2 + h), {"tok": peer2[h]})
                for h in range(2)
            ]
        elif name == "send3":
            for h in range(2):
                total = part2[p, h] + got2[step, p, h].astype(jnp.float32)
                part2[p, h] = total
                part3_bf[p, h] = total.astype(jnp.bfloat16)
            flying[c] = spread3(
                c, 4,
                lambda h, d: part3_bf.at[p, h, at(far[d] * r16, r16), :],
                lambda h, d: got3.at[step, p, h, d],
            )
        elif name == "change" or (name == "gather3" and step == 0):
            for h in range(2):
                total = part2[p, h, at(z * r16, r16), :]
                for d in range(n_z - 1):
                    total = total + got3[step, p, h, d].astype(jnp.float32)
                if step == 0:
                    fresh = initial(c, h) - total
                    shard[p, h] = fresh
                    weights[1, c, at(own3[h], r16), :] = fresh.astype(jnp.bfloat16)
                else:
                    change_mine[p, h] = (shard[p, h] - total) - initial(c, h)
            if step == 1:
                flying[c] = [
                    remote(change_mine.at[p], change_got.at[p], slot_of(c, 4 + 4 * n_z), {"order": 1 - place})
                ]
        if name == "gather3":
            if step == 1:
                for h in range(2):
                    earlier = jnp.where(place > 0, change_got[p, h], 0.0)
                    closing = initial(c, h) + earlier + change_mine[p, h]
                    weights[2, c, at(own3[h], r16), :] = closing.astype(jnp.bfloat16)
            flying[c] = spread3(
                c, 4 + 2 * (n_z - 1),
                lambda h, d: held.at[at(own3[h], r16), :],
                lambda h, d: held.at[at(own3[h], r16), :],
            )
        elif name in ("gather2", "gather1"):
            wide = name == "gather1"
            start, size = (own1, r128) if wide else (own2, r64)
            peer = peer1 if wide else peer2
            base = 4 + 4 * (n_z - 1) + (2 if wide else 0)
            flying[c] = [
                remote(held.at[at(start[h], size), :], held.at[at(start[h], size), :],
                       slot_of(c, base + h), {"tok": peer[h]})
                for h in range(2)
            ]

    def apply(step, c, part):
        if c == 0 and part == 0:
            loads[-1].wait()
        lines = slice(part * rows, (part + 1) * rows)
        rows_in = query[lines, :]
        both = jnp.dot(rows_in, weights[step, c, :, : 2 * cols], preferred_element_type=jnp.float32)
        gate, up = both[:, :cols], both[:, cols:]
        hidden = (jax.nn.silu(gate) * up).astype(jnp.bfloat16)
        result = lax.dot_general(
            hidden, weights[step, c, :, 2 * cols :], (((1,), (1,)), ((), ())), preferred_element_type=jnp.float32
        )
        if c > 0:
            result = y_part[lines, :] + result
        if c < CHUNKS - 1:
            y_part[lines, :] = result
            return
        norm_inv = lax.rsqrt(jnp.mean(result * result, axis=1, keepdims=True) + 1e-06)
        out_ref[lines, :] = (result * norm_inv * gain_ref[...]).astype(jnp.bfloat16)

    for op in plan():
        {"E": elementwise, "G": gradient, "S": advance, "Q": apply}[op[0]](*op[1:])


def fused(queries, key_tokens, value_tokens, learn_rates, fast_init, out_gain):
    tokens, width = key_tokens.shape
    n_tok = lax.axis_size("tok")
    n_z = n_tok // 4
    cols = width // CHUNKS
    deep = 3 * cols
    q = width // 8
    bf, f32 = jnp.bfloat16, jnp.float32
    factor = (tokens * n_tok) ** (-0.5)
    sems = CHUNKS * (8 + 4 * n_z)
    hbm = pl.BlockSpec(memory_space=pl.ANY)
    vmem = pl.BlockSpec(memory_space=pltpu.VMEM)
    return pl.pallas_call(
        functools.partial(fused_kernel, factor),
        out_shape=jax.ShapeDtypeStruct((tokens, width), bf),
        in_specs=[hbm, hbm, vmem, hbm, vmem, hbm],
        out_specs=vmem,
        scratch_shapes=[
            pltpu.VMEM((width, tokens), bf),
            pltpu.VMEM((tokens, width), bf),
            pltpu.VMEM((width, tokens), bf),
            pltpu.VMEM((tokens, deep), bf),
            pltpu.VMEM((3, CHUNKS, width, deep), bf),
            pltpu.VMEM((CHUNKS, 2, q // n_z, deep), f32),
            pltpu.VMEM((CHUNKS, width, cols), f32),
            pltpu.VMEM((CHUNKS, width, deep), f32),
            pltpu.VMEM((CHUNKS, width, deep), bf),
            pltpu.VMEM((CHUNKS, 2, q, deep), f32),
            pltpu.VMEM((CHUNKS, 2, q, deep), bf),
            pltpu.VMEM((CHUNKS, 2, q, deep), bf),
            pltpu.VMEM((2, CHUNKS, 2, 2 * q, deep), bf),
            pltpu.VMEM((2, CHUNKS, 2, q, deep), bf),
            pltpu.VMEM((2, CHUNKS, 2, n_z - 1, q // n_z, deep), bf),
            pltpu.VMEM((CHUNKS, 2, q // n_z, deep), f32),
            pltpu.VMEM((CHUNKS, 2, q // n_z, deep), f32),
            pltpu.VMEM((tokens, width), bf),
            pltpu.VMEM((tokens, width), bf),
            pltpu.VMEM((width, 3 * width), f32),
            pltpu.VMEM((tokens, width), bf),
            pltpu.VMEM((tokens, width), f32),
            pltpu.SemaphoreType.DMA((2 + 2 * PARTS,)),
            pltpu.SemaphoreType.DMA((sems,)),
            pltpu.SemaphoreType.DMA((sems,)),
        ],
        compiler_params=pltpu.CompilerParams(
            collective_id=0, has_side_effects=True, vmem_limit_bytes=67043328
        ),
    )(
        key_tokens, value_tokens, learn_rates.reshape(-1, 128), fast_init,
        out_gain.reshape(1, -1), queries,
    )


def solution(mesh):
    return jax.shard_map(
        fused if tiles(mesh) else shards,
        mesh=mesh,
        in_specs=(
            P(("order", "tok"), None),
            P(("order", "tok"), None),
            P(("order", "tok"), None),
            P(("order", "tok")),
            P(),
            P(),
        ),
        out_specs=P(("order", "tok"), None),
        check_vma=False,
    )
```
